32 devices in a mesh: cell: 8 (over z, x), patch: 4 (over y, core).
Axes of the slice: x: 2, y: 2, z: 4, core: 2. Of those that a mesh axis runs over, the one named last changes fastest.
Arguments:
- right_side: float32 [256, 3, 2112], P('cell', None, 'patch'), may hold values from -45 to 45
- analysis: float32 [2112, 1089], P('patch'), may hold values from -0.125 to 0.125
- spectral: float32 [256, 1089], P('cell'), may hold values from 0.1 to 10
- near_kernel: float32 [2112, 2112], P(None, 'patch'), may hold values from -0.125 to 0.125
- near_send: int32 [8, 8, 8], P('cell'), may hold values from 0 to 31, as said below
- near_target: int32 [8, 8, 8], P('cell'), may hold values from -1 to 31, as said below
- near_strength: float32 [8, 8, 8], P('cell'), may hold values from 0.2 to 1
Outputs:
- solution: float32 [256, 3, 2112], P('cell', None, 'patch')
- relative_residual: float32 [], replicated
The draws below stay inside these ranges and needn't reach their ends.
Inputs may be any that keep to these rules, and one draw needn't show every extreme that they name: `near_send`: each entry names one of the 32 cells of the sending group. Slot s of near_send[d, q] pairs with slot s of near_target[q, d]. Live slots come first. From group d to a group q at index distance at most one modulo 8 (d itself included) at most 8 slots are live, to any other group at most 2; both bounds are reached in every draw.
All inputs are finite; a program needn't handle non-finite values.
Results may differ from the reference program's by a relative error of at most 0.0003.
Values sent between devices are 32-bit elements; how exact they have to be, the bound alone decides.
A program may use at most 128 MiB of HBM per device.

```python
import math
import jax
import jax.numpy as jnp
from jax import lax

PTS = 2112
COEF = 1089
CELL_DEV = 32
CAP = 8
FAR_CAP = 2
ITERS = 8
GROUPS = 8
NCELLS = 256


def near_lists(key):
    keys = jax.random.split(jax.random.fold_in(key, 11), 6)
    sender = jnp.arange(GROUPS, dtype=jnp.int32)[:, None]
    receiver = jnp.arange(GROUPS, dtype=jnp.int32)[None, :]
    forward_gap = (receiver - sender) % GROUPS
    backward_gap = (sender - receiver) % GROUPS
    distance = jnp.minimum(forward_gap, backward_gap)
    close_count = jax.random.randint(keys[0], (GROUPS, GROUPS), CAP // 2, CAP + 1)
    far_count = jax.random.randint(keys[1], (GROUPS, GROUPS), 0, FAR_CAP + 1)
    counts = jnp.where(distance <= 1, close_count, far_count)
    full_pick = jax.random.randint(keys[2], (GROUPS, 1), 0, 3)
    full_peer = (sender + full_pick - 1 + GROUPS) % GROUPS
    counts = jnp.where(receiver == full_peer, CAP, counts)
    far_offset = jax.random.randint(keys[3], (GROUPS, 1), 2, GROUPS - 1)
    far_peer = (sender + far_offset) % GROUPS
    counts = jnp.where(receiver == far_peer, FAR_CAP, counts)
    send_cells = jax.random.randint(keys[4], (GROUPS, GROUPS, CAP), 0, CELL_DEV).astype(jnp.int32)
    raw_targets = jax.random.randint(keys[5], (GROUPS, GROUPS, CAP), 0, CELL_DEV)
    slot_ids = jnp.arange(CAP, dtype=jnp.int32)[None, None, :]
    live = slot_ids < counts[:, :, None]
    targets = jnp.where(live, raw_targets, -1).astype(jnp.int32)
    return (send_cells, jnp.transpose(targets, (1, 0, 2)))


def draw_near_send(key, part):
    return near_lists(key)[0]


def draw_near_target(key, part):
    return near_lists(key)[1]


def draw_right_side(key, part):
    keys = jax.random.split(jax.random.fold_in(key, 5), 2)
    base = jax.random.truncated_normal(keys[0], -4.0, 4.0, (NCELLS, 3, PTS), jnp.float32)
    rough = jnp.exp(jax.random.uniform(keys[1], (NCELLS, 1, 1), jnp.float32) * math.log(10.0))
    rising = (3.0 ** (jnp.arange(NCELLS, dtype=jnp.float32) / NCELLS)).reshape(NCELLS, 1, 1)
    return (0.3 * base * rough * rising).astype(jnp.float32)


def block_levels(rng, shape, shards, least, top_value):
    level = 1.0
    for axis_at, shards_of in shards:
        draws = jax.random.uniform(jax.random.fold_in(jax.random.fold_in(rng, 6), axis_at), (shards_of,), jnp.float32, least / len(shards), top_value / len(shards))
        level = level * jnp.repeat(jnp.exp(draws), shape[axis_at] // shards_of).reshape((-1,) + (1,) * (len(shape) - 1 - axis_at))
    return level


def gaussian(stream_key, dims, width, bound, shards=(), kind=jnp.bfloat16):
    factor_of = block_levels(stream_key, dims, shards, -0.22, 0.18) if shards else 1.0
    drawn = jax.random.normal(stream_key, dims, jnp.float32) * width * factor_of
    return jnp.minimum(jnp.maximum(drawn, -bound), bound).astype(kind)


def setup_inputs(seed: int = 0) -> dict:
    key_list = jax.random.split(jax.random.key(seed), 8)
    right_side = draw_right_side(jax.random.fold_in(key_list[7], 71), 0)
    analysis = gaussian(key_list[1], (PTS, COEF), PTS ** -0.5, 0.125, ((0, 4),), jnp.float32)
    spectral = jnp.clip(jnp.exp(math.log(10.0) - 4.6051702 * jax.random.uniform(key_list[2], (NCELLS, COEF), jnp.float32) ** block_levels(key_list[2], (NCELLS, COEF), ((0, 8),), -0.2, 0.2)), 0.1, 10.0)
    near_kernel = gaussian(key_list[3], (PTS, PTS), PTS ** -0.5, 0.125, ((1, 4),), jnp.float32)
    near_send = draw_near_send(jax.random.fold_in(key_list[7], 71), 0)
    near_target = draw_near_target(jax.random.fold_in(key_list[7], 71), 0)
    near_strength = jnp.clip(jnp.exp(math.log(1.0) - 1.609438 * jax.random.uniform(key_list[6], (GROUPS, GROUPS, CAP), jnp.float32) ** block_levels(key_list[6], (GROUPS, GROUPS, CAP), ((0, 8),), -0.2, 0.2)), 0.2, 1.0)
    return {"right_side": right_side, "analysis": analysis, "spectral": spectral, "near_kernel": near_kernel, "near_send": near_send, "near_target": near_target, "near_strength": near_strength}


HIGH_PRECISION = lax.Precision.HIGHEST

def small_solve(gram, right):
    lower = jnp.linalg.cholesky(gram)
    order = gram.shape[0]
    forward = []
    for row in range(order):
        value = right[row] - sum((lower[row, col] * forward[col] for col in range(row)))
        forward.append(value / lower[row, row])
    backward = [None] * order
    for row in reversed(range(order)):
        value = forward[row] - sum((lower[col, row] * backward[col] for col in range(row + 1, order)))
        backward[row] = value / lower[row, row]
    return jnp.stack(backward)

def apply_operator(vector, analysis, spectral, near_kernel, source_rows, target_cells, weights):

    def one_group(inputs):
        sources, targets, strengths = inputs
        blocks = vector[sources] * strengths[:, None, None]
        return jax.ops.segment_sum(blocks, jnp.maximum(targets, 0), num_segments=CELL_DEV)
    gathered = lax.map(one_group, (source_rows, target_cells, weights)).reshape(NCELLS, 3, PTS)
    coefficients = jnp.einsum('ncp,pk->nck', vector, analysis, precision=HIGH_PRECISION)
    self_term = jnp.einsum('nck,pk->ncp', coefficients * spectral[:, None, :], analysis, precision=HIGH_PRECISION)
    near_term = jnp.einsum('ncp,pq->ncq', gathered, near_kernel, precision=HIGH_PRECISION)
    return vector + self_term + near_term

def reference(right_side, analysis, spectral, near_kernel, near_send, near_target, near_strength):
    group_ids = jnp.arange(GROUPS, dtype=jnp.int32)
    source_rows = (group_ids[None, :, None] * CELL_DEV + jnp.transpose(near_send, (1, 0, 2))).astype(jnp.int32)
    source_rows = source_rows.reshape(GROUPS, GROUPS * CAP)
    target_cells = near_target.reshape(GROUPS, GROUPS * CAP)
    weights = jnp.where(near_target >= 0, near_strength, jnp.zeros_like(near_strength)).reshape(GROUPS, GROUPS * CAP)
    beta = jnp.sqrt(jnp.sum(right_side * right_side))
    basis = [right_side / beta]
    hessen = jnp.zeros((ITERS + 1, ITERS), jnp.float32)
    for column in range(ITERS):
        image = apply_operator(basis[column], analysis, spectral, near_kernel, source_rows, target_cells, weights)
        projected = jnp.stack([jnp.sum(earlier * image) for earlier in basis])
        image = image - sum((projected[member] * basis[member] for member in range(column + 1)))
        length = jnp.sqrt(jnp.sum(image * image))
        hessen = hessen.at[:column + 1, column].set(projected)
        hessen = hessen.at[column + 1, column].set(length)
        basis.append(image / length)
    gram = jnp.dot(hessen.T, hessen, precision=HIGH_PRECISION)
    coeffs = small_solve(gram, beta * hessen[0])
    solution = sum((coeffs[member] * basis[member] for member in range(ITERS)))
    target_vec = jnp.zeros((ITERS + 1,), jnp.float32).at[0].set(beta)
    misfit = target_vec - jnp.dot(hessen, coeffs, precision=HIGH_PRECISION)
    relative_residual = jnp.sqrt(jnp.sum(misfit * misfit)) / beta
    return (solution, relative_residual)
```

```python
import functools

import jax
import jax.numpy as jnp
from jax import lax
from jax.experimental import pallas as pl
from jax.experimental.pallas import tpu as pltpu
from jax.sharding import PartitionSpec as P

ITERS = 8
FAR_CAP = 2
LANES = 128
MSG = 16
F32 = jnp.float32
BF16 = jnp.bfloat16
MESH = pl.DeviceIdType.MESH


def round_up(value, unit):
    return -(-value // unit) * unit


def split(x):
    hi = x.astype(BF16)
    return hi, (x - hi.astype(F32)).astype(BF16)


def halves(x):
    return x[:, :LANES] + x[:, LANES:]


def dot(a, b):
    return jnp.dot(a, b, preferred_element_type=F32)


def product(hi, lo, b):
    rows = hi.shape[0]
    cut = round_up(rows // 2, 16)
    return jnp.concatenate(
        [halves(dot(hi[a:z], b) + dot(lo[a:z], b)) for a, z in ((0, cut), (cut, rows))], 0
    )


def dot_nt(a, b):
    return lax.dot_general(a, b, (((1,), (1,)), ((), ())), preferred_element_type=F32)


def dot_tn(a, b):
    return lax.dot_general(a, b, (((0,), (0,)), ((), ())), preferred_element_type=F32)


def blocks_of(groups, near_rows, far_rows):
    out, at = {}, 0
    for d in sorted(range(groups), key=lambda d: (min(d, groups - d) > 1, d)):
        rows = near_rows if min(d, groups - d) <= 1 else far_rows
        out[d] = (at, rows)
        at += rows
    return out, at


def packed_rows(rows):
    return round_up(rows * 3 // 4, 8)


def pack(dst, x, lanes):
    idle = LANES - lanes
    main = dst.shape[0]
    tail = x.shape[0] - main
    lane = lax.broadcasted_iota(jnp.int32, (1, LANES), 1)
    dst[...] = x[:main]
    for i in range(lanes // idle):
        rows = slice(i * tail, (i + 1) * tail)
        moved = pltpu.roll(x[main:], lanes - idle * i, 1)
        dst[rows, :] = jnp.where(lane >= lanes, moved, x[rows])


def unpack(src, total, lanes):
    idle = LANES - lanes
    main = src.shape[0]
    tail = total - main
    lane = lax.broadcasted_iota(jnp.int32, (1, LANES), 1)
    end = jnp.zeros((tail, LANES), F32)
    for i in range(lanes // idle):
        moved = pltpu.roll(src[i * tail : (i + 1) * tail], (idle * i - lanes) % LANES, 1)
        end = jnp.where((lane >= idle * i) & (lane < idle * (i + 1)), moved, end)
    return jnp.concatenate((jnp.where(lane < lanes, src, 0.0), end), 0)


def pieces_of(rows):
    return next(n for n in (2, 1) if rows // 8 % n == 0)


def tile_rows(total, unit, most):
    best = unit
    for rows in range(unit, most + 1, unit):
        if total % rows == 0:
            best = rows
    return best


def kernel(
    groups, patches, lanes, blocks,
    u0, kernel_t, amine, aother, bmat, spec, sel, mix,
    out, res,
    raw, fresh, packed, basis, vs, cs, pair, khi, klo, ahi, alo, bhi, blo, part_out, part_in, half_out, half_in,
    sendrows, recvrows, msg1, msg2, hess, hrows,
    ag_send, ag_recv, fw_send, fw_recv, s1_send, s1_recv, s2_send, s2_recv, a2_send, a2_recv,
    cf_send, cf_recv, ex_send, ex_recv, sw_send, sw_recv,
):
    points = u0.shape[0]
    half = spec.shape[1]
    main = packed.shape[2]
    pieces = pieces_of(main)
    chunk = main // pieces
    width = 2 * points
    g = lax.axis_index("cell")
    p = lax.axis_index("patch")
    core = lax.rem(p, 2)
    chip = p // 2
    sib = p + 1 - 2 * core
    chips = patches // 2

    msg1[...] = jnp.zeros_like(msg1)
    barrier = pltpu.get_barrier_semaphore()
    for d in range(1, groups):
        pl.semaphore_signal(barrier, inc=1, device_id=(lax.rem(g + d, groups), p), device_id_type=MESH)
    for d in range(1, patches):
        pl.semaphore_signal(barrier, inc=1, device_id=(g, lax.rem(p + d, patches)), device_id_type=MESH)

    hess[...] = jnp.zeros_like(hess)
    raw[0] = u0[...]
    pl.semaphore_wait(barrier, groups + patches - 2)

    swap = pltpu.make_async_remote_copy(
        src_ref=aother, dst_ref=pair.at[core],
        send_sem=sw_send.at[0], recv_sem=sw_recv.at[0],
        device_id=(g, sib), device_id_type=MESH,
    )
    swap.start()
    for c in range(chips):
        khi[c], klo[c] = split(kernel_t[:, c * width : (c + 1) * width])
    for c in range(2):
        bhi[c], blo[c] = split(bmat[:, c * half : (c + 1) * half])
    pair[core] = amine[...]
    swap.wait()
    ahi[...], alo[...] = split(pair[...].reshape(width, half).T)

    def dots(slot, count):
        def one(i, carry):
            msg1[slot, g, pl.ds(i, 1), :] = jnp.sum(basis[i] * raw[count], axis=0, keepdims=True)
            return carry

        lax.fori_loop(0, count, one, 0)
        msg1[slot, g, ITERS : ITERS + 1, :] = jnp.sum(raw[count] * raw[count], axis=0, keepdims=True)

    def stage1(slot):
        return [
            pltpu.make_async_remote_copy(
                src_ref=msg1.at[slot, g], dst_ref=msg1.at[slot, g],
                send_sem=s1_send.at[slot, d], recv_sem=s1_recv.at[slot, d],
                device_id=(lax.rem(g + d, groups), p), device_id_type=MESH,
            )
            for d in range(1, groups)
        ]

    def stage2(slot):
        return [
            pltpu.make_async_remote_copy(
                src_ref=msg2.at[slot, p], dst_ref=msg2.at[slot, p],
                send_sem=s2_send.at[slot, d], recv_sem=s2_recv.at[slot, d],
                device_id=(g, lax.rem(p + d, patches)), device_id_type=MESH,
            )
            for d in range(1, patches)
        ]

    def relay_sums(slot, first):
        for c in first:
            c.wait()
        local = msg1[slot, 0]
        for q in range(1, groups):
            local = local + msg1[slot, q]
        msg2[slot, p] = local
        second = stage2(slot)
        for c in second:
            c.start()
        return second

    def finish_sums(slot, second):
        for c in second:
            c.wait()
        whole = msg2[slot, 0]
        for q in range(1, patches):
            whole = whole + msg2[slot, q]
        return jnp.sum(whole, axis=1, keepdims=True)

    row_ids = lax.broadcasted_iota(jnp.int32, (MSG, 1), 0)
    lane_ids = lax.broadcasted_iota(jnp.int32, (1, LANES), 1)

    def record(step, sums):
        squared = sums[ITERS : ITERS + 1, :]
        h = jnp.where(row_ids < ITERS, sums, 0.0)
        length = jnp.sqrt(squared - jnp.sum(h * h, axis=0, keepdims=True))
        column = jnp.where(row_ids == step, length, h)
        lane = lax.rem(step + ITERS, ITERS + 1)
        hess[...] = jnp.where(lane_ids == lane, column, hess[...])
        return h, length

    vrows = tile_rows(points, 8, 96)

    def body(step, carry):
        slot = lax.rem(step, 2)
        pack(packed.at[slot, p], raw[step], lanes)
        own = pltpu.make_async_remote_copy(
            src_ref=packed.at[slot, p], dst_ref=packed.at[slot, p],
            send_sem=ag_send.at[slot, 0, 0], recv_sem=ag_recv.at[slot, 0, 0],
            device_id=(g, sib), device_id_type=MESH,
        )
        cross, forward = [], []
        for n in range(pieces):
            rows = pl.ds(n * chunk, chunk)
            for k in range(1, chips):
                cross.append(pltpu.make_async_remote_copy(
                    src_ref=packed.at[slot, p, rows], dst_ref=packed.at[slot, p, rows],
                    send_sem=ag_send.at[slot, k, n], recv_sem=ag_recv.at[slot, k, n],
                    device_id=(g, lax.rem(p + 2 * k, patches)), device_id_type=MESH,
                ))
                src = lax.rem(p + patches - 2 * k, patches)
                forward.append(pltpu.make_async_remote_copy(
                    src_ref=packed.at[slot, src, rows], dst_ref=packed.at[slot, src, rows],
                    send_sem=fw_send.at[slot, k, n], recv_sem=fw_recv.at[slot, k, n],
                    device_id=(g, sib), device_id_type=MESH,
                ))
        for c in cross:
            c.start()
        own.start()
        dots(slot, step)
        first = stage1(slot)
        for c in first:
            c.start()

        def put(who, v):
            rows = pl.ds(pl.multiple_of(who * points, 16), points)
            hi, lo = split(v)
            vs[rows, :LANES] = hi
            vs[rows, LANES:] = lo

        def place(who):
            put(who, unpack(packed[slot, who], points, lanes))

        def wide(which):
            return vs[pl.ds(pl.multiple_of(which * width, 16), width), :]

        put(p, raw[step])
        own.wait()
        place(sib)
        near = wide(chip)
        pack(part_out.at[slot], product(ahi, alo, near), lanes)
        partials = [
            pltpu.make_async_remote_copy(
                src_ref=part_out.at[slot], dst_ref=part_in.at[slot, k - 1],
                send_sem=cf_send.at[slot, k], recv_sem=cf_recv.at[slot, k],
                device_id=(g, lax.rem(p + 2 * k, patches)), device_id_type=MESH,
            )
            for k in range(1, chips)
        ]
        for c in partials:
            c.start()
        acc = product(khi.at[chip], klo.at[chip], near)
        for c, f in zip(cross, forward):
            c.wait()
            f.start()
        for k in range(1, chips):
            place(lax.rem(p + patches - 2 * k, patches))
        for f in forward:
            f.wait()
        for k in range(1, chips):
            other = lax.rem(chip + chips - k, chips)
            place(2 * other + 1 - core)
            acc = acc + product(khi.at[other], klo.at[other], wide(other))
        whi, wlo = split(acc)
        sendrows[slot] = dot_nt(sel[...], whi) + dot_nt(sel[...], wlo)
        sends = []
        for d in sorted(range(1, groups), key=lambda d: min(d, groups - d) > 1):
            at, rows = blocks[d]
            sends.append(pltpu.make_async_remote_copy(
                src_ref=sendrows.at[slot, pl.ds(at, rows)], dst_ref=recvrows.at[slot, pl.ds(at, rows)],
                send_sem=a2_send.at[slot, d], recv_sem=a2_recv.at[slot, d],
                device_id=(lax.rem(g + d, groups), p), device_id_type=MESH,
            ))
        for c in sends:
            c.start()
        second = relay_sums(slot, first)
        recvrows[slot, : blocks[0][1], :] = sendrows[slot, : blocks[0][1], :]

        coef = part_out[slot]
        for k, c in enumerate(partials, 1):
            c.wait()
            coef = coef + part_in[slot, k - 1]
        half_out[slot] = coef
        exchange = pltpu.make_async_remote_copy(
            src_ref=half_out.at[slot], dst_ref=half_in.at[slot],
            send_sem=ex_send.at[slot], recv_sem=ex_recv.at[slot],
            device_id=(g, sib), device_id_type=MESH,
        )
        exchange.start()

        def self_half(which, values):
            hi, lo = split(values)
            cs[:, :LANES] = hi
            cs[:, LANES:] = lo
            return product(bhi.at[which], blo.at[which], cs[...])

        fresh[...] = raw[step] + self_half(core, unpack(coef, half, lanes) * spec[core])
        h, length = record(step, finish_sums(slot, second))
        scale = jnp.broadcast_to(1.0 / length, (1, LANES))
        hrows[...] = jnp.broadcast_to(h, (MSG, LANES))

        @pl.loop(0, points // vrows)
        def _(t):
            rows = pl.ds(pl.multiple_of(t * vrows, 8), vrows)

            def one(i, pair):
                c = hrows[pl.ds(i, 1), :]
                return pair[0] - c * basis[i, rows, :], pair[1] - c * raw[i + 1, rows, :]

            v, z = lax.fori_loop(0, step, one, (raw[step, rows, :], fresh[rows, :]))
            basis[step, rows, :] = v * scale
            fresh[rows, :] = z

        exchange.wait()
        fresh[...] += self_half(1 - core, unpack(half_in[slot], half, lanes) * spec[1 - core])
        mixes = jnp.concatenate(split(mix[...]), 1)
        for c in sends:
            c.wait()
        rhi, rlo = split(recvrows[slot])
        raw[step + 1] = (fresh[...] + halves(dot_tn(rhi, mixes) + dot_tn(rlo, mixes))) * scale
        return carry

    lax.fori_loop(0, ITERS, body, 0)

    slot = ITERS % 2
    dots(slot, ITERS)
    first = stage1(slot)
    for c in first:
        c.start()
    record(ITERS, finish_sums(slot, relay_sums(slot, first)))

    work = hess[...]
    beta = work[0:1, ITERS : ITERS + 1]
    rows = []
    for k in range(ITERS):
        col = work[:, k : k + 1]
        prods = jnp.sum(col * work, axis=0, keepdims=True)
        row = prods / prods[:, k : k + 1]
        rows.append(jnp.where(lane_ids >= k, row, 0.0))
        work = work - jnp.where(lane_ids >= k, col * row, 0.0)
    y = jnp.where(lane_ids == ITERS, -1.0, jnp.zeros((1, LANES), F32))
    for k in reversed(range(ITERS)):
        value = -jnp.sum(rows[k] * y, axis=1, keepdims=True)
        y = jnp.where(lane_ids == k, value, y)
    answer = y[:, 0:1] * basis[0]
    for k in range(1, ITERS):
        answer = answer + y[:, k : k + 1] * basis[k]
    out[...] = answer
    left = work[:, ITERS : ITERS + 1]
    norm = jnp.sqrt(jnp.sum(left * left, axis=0, keepdims=True)) / beta
    res[...] = jnp.broadcast_to(norm, res.shape)


def per_device(groups, patches, right_side, analysis, spectral, near_kernel, near_send, near_target, near_strength):
    cells, comps, points = right_side.shape
    total = near_kernel.shape[0]
    modes = analysis.shape[1]
    lanes = cells * comps
    cap = near_send.shape[-1]
    low = modes // 2
    half = round_up(modes - low, 16)
    pad = LANES - lanes
    near_rows, far_rows = cap * comps, round_up(FAR_CAP * comps, 8)
    blocks, total_rows = blocks_of(groups, near_rows, far_rows)
    g = lax.axis_index("cell")
    core = lax.rem(lax.axis_index("patch"), 2)

    u0 = jnp.pad(right_side.reshape(lanes, points).T, ((0, 0), (0, pad)))
    kernel_t = near_kernel.T

    def two_halves(x, axis):
        def padded(piece):
            pads = [(0, 0)] * x.ndim
            pads[axis] = (0, half - piece.shape[axis])
            return jnp.pad(piece, pads)

        return (
            padded(lax.slice_in_dim(x, 0, low, axis=axis)),
            padded(lax.slice_in_dim(x, low, modes, axis=axis)),
        )

    first, second = two_halves(analysis, 1)
    bmat = jnp.concatenate((first, second), 1)
    amine = jnp.where(core == 0, first, second)
    aother = jnp.where(core == 0, second, first)
    spec_first, spec_second = two_halves(spectral, 1)
    spec = jnp.stack((spec_first.T, spec_second.T))
    spec = jnp.pad(jnp.repeat(spec, comps, axis=2), ((0, 0), (0, 0), (0, pad)))

    def slot_rows(x, fill):
        close = jnp.concatenate((x[:2], x[groups - 1 :]), 0)
        far = x[2 : groups - 1, :FAR_CAP]
        close = jnp.broadcast_to(close[:, :, None], close.shape + (comps,)).reshape(-1)
        far = jnp.broadcast_to(far[:, :, None], far.shape + (comps,)).reshape(-1, FAR_CAP * comps)
        far = jnp.pad(far, ((0, 0), (0, far_rows - FAR_CAP * comps)), constant_values=fill).reshape(-1)
        return jnp.concatenate((close, far))[:, None]

    def ahead(x):
        return lax.dynamic_slice_in_dim(jnp.concatenate((x, x), 0), g, groups, 0)

    def behind(x):
        return lax.dynamic_slice_in_dim(jnp.concatenate((x, x), 0), g + 1, groups, 0)[::-1]

    row_comp = jnp.concatenate((
        jnp.tile(jnp.arange(comps), 3 * cap),
        jnp.tile(jnp.pad(jnp.tile(jnp.arange(comps), FAR_CAP), (0, far_rows - FAR_CAP * comps), constant_values=-1), groups - 3),
    ))[:, None]
    lane = jnp.arange(LANES)[None, :]
    same = (row_comp == lane % comps) & (lane < lanes)
    sel = (same & (slot_rows(ahead(near_send[0]), -1) == lane // comps)).astype(BF16)
    hit = same & (slot_rows(behind(near_target[0]), -1) == lane // comps)
    mix = jnp.where(hit, slot_rows(behind(near_strength[0]), 0.0), 0.0)

    vmem = pl.BlockSpec(memory_space=pltpu.VMEM)
    dma = pltpu.SemaphoreType.DMA
    chips = max(patches // 2, 1)
    main = packed_rows(points)
    pieces = pieces_of(main)
    answer, residual = pl.pallas_call(
        functools.partial(kernel, groups, patches, lanes, blocks),
        out_shape=(
            jax.ShapeDtypeStruct((points, LANES), F32),
            jax.ShapeDtypeStruct((8, LANES), F32),
        ),
        in_specs=[vmem] * 8,
        out_specs=(vmem, vmem),
        scratch_shapes=[
            pltpu.VMEM((ITERS + 1, points, LANES), F32),
            pltpu.VMEM((points, LANES), F32),
            pltpu.VMEM((2, patches, main, LANES), F32),
            pltpu.VMEM((ITERS, points, LANES), F32),
            pltpu.VMEM((total, 2 * LANES), BF16),
            pltpu.VMEM((half, 2 * LANES), BF16),
            pltpu.VMEM((2, points, half), F32),
            pltpu.VMEM((chips, points, 2 * points), BF16),
            pltpu.VMEM((chips, points, 2 * points), BF16),
            pltpu.VMEM((half, 2 * points), BF16),
            pltpu.VMEM((half, 2 * points), BF16),
            pltpu.VMEM((2, points, half), BF16),
            pltpu.VMEM((2, points, half), BF16),
            pltpu.VMEM((2, packed_rows(half), LANES), F32),
            pltpu.VMEM((2, max(chips - 1, 1), packed_rows(half), LANES), F32),
            pltpu.VMEM((2, packed_rows(half), LANES), F32),
            pltpu.VMEM((2, packed_rows(half), LANES), F32),
            pltpu.VMEM((2, total_rows, points), F32),
            pltpu.VMEM((2, total_rows, points), F32),
            pltpu.VMEM((2, groups, MSG, LANES), F32),
            pltpu.VMEM((2, patches, MSG, LANES), F32),
            pltpu.VMEM((MSG, LANES), F32),
            pltpu.VMEM((MSG, LANES), F32),
            dma((2, chips, pieces)), dma((2, chips, pieces)), dma((2, chips, pieces)), dma((2, chips, pieces)),
            dma((2, groups)), dma((2, groups)), dma((2, patches)), dma((2, patches)),
            dma((2, groups)), dma((2, groups)),
            dma((2, chips)), dma((2, chips)), dma((2,)), dma((2,)), dma((1,)), dma((1,)),
        ],
        compiler_params=pltpu.CompilerParams(
            collective_id=0, has_side_effects=True, vmem_limit_bytes=60 * 1024 * 1024
        ),
        name="gmres",
    )(u0, kernel_t, amine, aother, bmat, spec, sel, mix)
    solution = answer[:, :lanes].T.reshape(cells, comps, points)
    return solution, residual[0, 0]


def solution(mesh):
    placed = (
        P("cell", None, "patch"),
        P("patch", None),
        P("cell", None),
        P(None, "patch"),
        P("cell", None, None),
        P("cell", None, None),
        P("cell", None, None),
    )
    return jax.shard_map(
        functools.partial(per_device, mesh.shape["cell"], mesh.shape["patch"]),
        mesh=mesh,
        in_specs=placed,
        out_specs=(P("cell", None, "patch"), P()),
        check_vma=False,
    )
```

```python
import functools

import jax
import jax.numpy as jnp
from jax import lax
from jax.experimental import pallas as pl
from jax.experimental.pallas import tpu as pltpu
from jax.sharding import PartitionSpec as P

ITERS = 8
FAR_CAP = 2
LANES = 128
MSG = 16
F32 = jnp.float32
BF16 = jnp.bfloat16
MESH = pl.DeviceIdType.MESH


def round_up(value, unit):
    return -(-value // unit) * unit


def split(x):
    hi = x.astype(BF16)
    return hi, (x - hi.astype(F32)).astype(BF16)


def halves(x):
    return x[:, :LANES] + x[:, LANES:]


def dot(a, b):
    return jnp.dot(a, b, preferred_element_type=F32)


def product(hi, lo, b):
    rows = hi.shape[0]
    cut = round_up(rows // 2, 16)
    return jnp.concatenate(
        [halves(dot(hi[a:z], b) + dot(lo[a:z], b)) for a, z in ((0, cut), (cut, rows))], 0
    )


def dot_nt(a, b):
    return lax.dot_general(a, b, (((1,), (1,)), ((), ())), preferred_element_type=F32)


def dot_tn(a, b):
    return lax.dot_general(a, b, (((0,), (0,)), ((), ())), preferred_element_type=F32)


def blocks_of(groups, near_rows, far_rows):
    out, at = {}, 0
    for d in sorted(range(groups), key=lambda d: (min(d, groups - d) > 1, d)):
        rows = near_rows if min(d, groups - d) <= 1 else far_rows
        out[d] = (at, rows)
        at += rows
    return out, at


def packed_rows(rows):
    return round_up(rows * 3 // 4, 8)


def pack(dst, x, lanes):
    idle = LANES - lanes
    main = dst.shape[0]
    tail = x.shape[0] - main
    lane = lax.broadcasted_iota(jnp.int32, (1, LANES), 1)
    dst[...] = x[:main]
    for i in range(lanes // idle):
        rows = slice(i * tail, (i + 1) * tail)
        moved = pltpu.roll(x[main:], lanes - idle * i, 1)
        dst[rows, :] = jnp.where(lane >= lanes, moved, x[rows])


def unpack(src, total, lanes):
    idle = LANES - lanes
    main = src.shape[0]
    tail = total - main
    lane = lax.broadcasted_iota(jnp.int32, (1, LANES), 1)
    end = jnp.zeros((tail, LANES), F32)
    for i in range(lanes // idle):
        moved = pltpu.roll(src[i * tail : (i + 1) * tail], (idle * i - lanes) % LANES, 1)
        end = jnp.where((lane >= idle * i) & (lane < idle * (i + 1)), moved, end)
    return jnp.concatenate((jnp.where(lane < lanes, src, 0.0), end), 0)


def low_modes(modes):
    return max(modes // 2 // LANES * LANES, 0)


def pieces_of(rows):
    return next(n for n in (2, 1) if rows // 8 % n == 0)


def tile_rows(total, unit, most):
    best = unit
    for rows in range(unit, most + 1, unit):
        if total % rows == 0:
            best = rows
    return best


def kernel(
    groups, patches, lanes, blocks,
    side, analysis, spectral, kernel_t, near_send, near_target, near_strength,
    out, res,
    raw, fresh, packed, basis, vs, cs, astage, kstage, both, pair, spec, sel, mixes,
    khi, klo, ahi, alo, bhi, blo, part_out, part_in, half_out, half_in,
    sendrows, recvrows, msg1, msg2, hess, hrows,
    ag_send, ag_recv, fw_send, fw_recv, s1_send, s1_recv, s2_send, s2_recv, a2_send, a2_recv,
    cf_send, cf_recv, ex_send, ex_recv, sw_send, sw_recv, in_sem,
):
    points = side.shape[1]
    modes = analysis.shape[1]
    cells = spectral.shape[0]
    comps = lanes // cells
    low = low_modes(modes)
    half = spec.shape[1]
    main = packed.shape[2]
    pieces = pieces_of(main)
    chunk = main // pieces
    width = 2 * points
    g = lax.axis_index("cell")
    p = lax.axis_index("patch")
    core = lax.rem(p, 2)
    chip = p // 2
    sib = p + 1 - 2 * core
    chips = patches // 2

    loads = [
        pltpu.make_async_copy(analysis, astage, in_sem.at[0]),
        pltpu.make_async_copy(kernel_t, kstage, in_sem.at[1]),
    ]
    for c in loads:
        c.start()
    msg1[...] = jnp.zeros_like(msg1)
    barrier = pltpu.get_barrier_semaphore()
    for d in range(1, groups):
        pl.semaphore_signal(barrier, inc=1, device_id=(lax.rem(g + d, groups), p), device_id_type=MESH)
    for d in range(1, patches):
        pl.semaphore_signal(barrier, inc=1, device_id=(g, lax.rem(p + d, patches)), device_id_type=MESH)

    hess[...] = jnp.zeros_like(hess)
    pad = jnp.zeros((LANES - lanes, points), F32)
    raw[0] = jnp.concatenate((side[...], pad), 0).T
    pl.semaphore_wait(barrier, groups + patches - 2)

    def slot_rows(ref, who, rows, fill):
        row = lax.broadcasted_iota(jnp.int32, (rows, ref.shape[1]), 0)
        slot = lax.broadcasted_iota(jnp.int32, (rows, ref.shape[1]), 1)
        count = rows // comps
        hit = (row // comps == slot) & (row < count * comps)
        values = jnp.broadcast_to(ref[pl.ds(who, 1), :].astype(F32), hit.shape)
        found = jnp.sum(jnp.where(hit, values, 0.0), axis=1, keepdims=True)
        return jnp.where(row[:, :1] < count * comps, found, fill)

    def setup():
        lane = lax.broadcasted_iota(jnp.int32, (1, LANES), 1)
        cell = (lane % cells).astype(F32)
        for d in range(groups):
            at, rows = blocks[d]
            row = lax.broadcasted_iota(jnp.int32, (rows, 1), 0)
            same = (row % comps == lane // cells) & (lane < lanes)
            ahead, behind = lax.rem(g + d, groups), lax.rem(g + groups - d, groups)
            picks = same & (slot_rows(near_send, ahead, rows, -1.0) == cell)
            sel[at : at + rows, :] = jnp.where(picks, 1.0, 0.0).astype(BF16)
            hits = same & (slot_rows(near_target, behind, rows, -1.0) == cell)
            mix = jnp.where(hits, slot_rows(near_strength, behind, rows, 0.0), 0.0)
            mixes[at : at + rows, :LANES], mixes[at : at + rows, LANES:] = split(mix)
        both[...] = jnp.zeros_like(both)
        spec[...] = jnp.zeros_like(spec)
        loads[0].wait()
        both[0, :, :low] = astage[:, :low]
        both[1, :, : modes - low] = astage[:, low:]
        swap = pltpu.make_async_remote_copy(
            src_ref=both.at[1 - core], dst_ref=pair.at[core],
            send_sem=sw_send.at[0], recv_sem=sw_recv.at[0],
            device_id=(g, sib), device_id_type=MESH,
        )
        swap.start()
        each = spectral[...]
        each = jnp.concatenate((each,) * comps + (jnp.zeros((LANES - lanes, modes), F32),), 0).T
        spec[0, :low, :] = each[:low]
        spec[1, : modes - low, :] = each[low:]
        for c in range(2):
            bhi[c], blo[c] = split(both[c])
        loads[1].wait()
        for c in range(chips):
            khi[c], klo[c] = split(kstage[:, c * width : (c + 1) * width])
        pair[core] = both[core]
        swap.wait()
        ahi[...], alo[...] = split(pair[...].reshape(width, half).T)

    def dots(slot, count):
        def one(i, carry):
            msg1[slot, g, pl.ds(i, 1), :] = jnp.sum(basis[i] * raw[count], axis=0, keepdims=True)
            return carry

        lax.fori_loop(0, count, one, 0)
        msg1[slot, g, ITERS : ITERS + 1, :] = jnp.sum(raw[count] * raw[count], axis=0, keepdims=True)

    def stage1(slot):
        return [
            pltpu.make_async_remote_copy(
                src_ref=msg1.at[slot, g], dst_ref=msg1.at[slot, g],
                send_sem=s1_send.at[slot, d], recv_sem=s1_recv.at[slot, d],
                device_id=(lax.rem(g + d, groups), p), device_id_type=MESH,
            )
            for d in range(1, groups)
        ]

    def stage2(slot):
        return [
            pltpu.make_async_remote_copy(
                src_ref=msg2.at[slot, p], dst_ref=msg2.at[slot, p],
                send_sem=s2_send.at[slot, d], recv_sem=s2_recv.at[slot, d],
                device_id=(g, lax.rem(p + d, patches)), device_id_type=MESH,
            )
            for d in range(1, patches)
        ]

    def relay_sums(slot, first):
        for c in first:
            c.wait()
        local = msg1[slot, 0]
        for q in range(1, groups):
            local = local + msg1[slot, q]
        msg2[slot, p] = local
        second = stage2(slot)
        for c in second:
            c.start()
        return second

    def finish_sums(slot, second):
        for c in second:
            c.wait()
        whole = msg2[slot, 0]
        for q in range(1, patches):
            whole = whole + msg2[slot, q]
        return jnp.sum(whole, axis=1, keepdims=True)

    row_ids = lax.broadcasted_iota(jnp.int32, (MSG, 1), 0)
    lane_ids = lax.broadcasted_iota(jnp.int32, (1, LANES), 1)

    def record(step, sums):
        squared = sums[ITERS : ITERS + 1, :]
        h = jnp.where(row_ids < ITERS, sums, 0.0)
        length = jnp.sqrt(squared - jnp.sum(h * h, axis=0, keepdims=True))
        column = jnp.where(row_ids == step, length, h)
        lane = lax.rem(step + ITERS, ITERS + 1)
        hess[...] = jnp.where(lane_ids == lane, column, hess[...])
        return h, length

    vrows = tile_rows(points, 8, 96)

    def body(step, carry):
        slot = lax.rem(step, 2)
        pack(packed.at[slot, p], raw[step], lanes)
        own = pltpu.make_async_remote_copy(
            src_ref=packed.at[slot, p], dst_ref=packed.at[slot, p],
            send_sem=ag_send.at[slot, 0, 0], recv_sem=ag_recv.at[slot, 0, 0],
            device_id=(g, sib), device_id_type=MESH,
        )
        cross, forward = [], []
        for n in range(pieces):
            rows = pl.ds(n * chunk, chunk)
            for k in range(1, chips):
                cross.append(pltpu.make_async_remote_copy(
                    src_ref=packed.at[slot, p, rows], dst_ref=packed.at[slot, p, rows],
                    send_sem=ag_send.at[slot, k, n], recv_sem=ag_recv.at[slot, k, n],
                    device_id=(g, lax.rem(p + 2 * k, patches)), device_id_type=MESH,
                ))
                src = lax.rem(p + patches - 2 * k, patches)
                forward.append(pltpu.make_async_remote_copy(
                    src_ref=packed.at[slot, src, rows], dst_ref=packed.at[slot, src, rows],
                    send_sem=fw_send.at[slot, k, n], recv_sem=fw_recv.at[slot, k, n],
                    device_id=(g, sib), device_id_type=MESH,
                ))
        for c in cross:
            c.start()
        own.start()
        dots(slot, step)
        first = stage1(slot)
        for c in first:
            c.start()

        pl.when(step == 0)(setup)

        def put(who, v):
            rows = pl.ds(pl.multiple_of(who * points, 16), points)
            hi, lo = split(v)
            vs[rows, :LANES] = hi
            vs[rows, LANES:] = lo

        def place(who):
            put(who, unpack(packed[slot, who], points, lanes))

        def wide(which):
            return vs[pl.ds(pl.multiple_of(which * width, 16), width), :]

        put(p, raw[step])
        own.wait()
        place(sib)
        near = wide(chip)
        pack(part_out.at[slot], product(ahi, alo, near), lanes)
        partials = [
            pltpu.make_async_remote_copy(
                src_ref=part_out.at[slot], dst_ref=part_in.at[slot, k - 1],
                send_sem=cf_send.at[slot, k], recv_sem=cf_recv.at[slot, k],
                device_id=(g, lax.rem(p + 2 * k, patches)), device_id_type=MESH,
            )
            for k in range(1, chips)
        ]
        for c in partials:
            c.start()
        acc = product(khi.at[chip], klo.at[chip], near)
        for c, f in zip(cross, forward):
            c.wait()
            f.start()
        for k in range(1, chips):
            place(lax.rem(p + patches - 2 * k, patches))
        for f in forward:
            f.wait()
        for k in range(1, chips):
            other = lax.rem(chip + chips - k, chips)
            place(2 * other + 1 - core)
            acc = acc + product(khi.at[other], klo.at[other], wide(other))
        whi, wlo = split(acc)
        sendrows[slot] = dot_nt(sel[...], whi) + dot_nt(sel[...], wlo)
        sends = []
        for d in sorted(range(1, groups), key=lambda d: min(d, groups - d) > 1):
            at, rows = blocks[d]
            sends.append(pltpu.make_async_remote_copy(
                src_ref=sendrows.at[slot, pl.ds(at, rows)], dst_ref=recvrows.at[slot, pl.ds(at, rows)],
                send_sem=a2_send.at[slot, d], recv_sem=a2_recv.at[slot, d],
                device_id=(lax.rem(g + d, groups), p), device_id_type=MESH,
            ))
        for c in sends:
            c.start()
        second = relay_sums(slot, first)
        recvrows[slot, : blocks[0][1], :] = sendrows[slot, : blocks[0][1], :]

        coef = part_out[slot]
        for k, c in enumerate(partials, 1):
            c.wait()
            coef = coef + part_in[slot, k - 1]
        half_out[slot] = coef
        exchange = pltpu.make_async_remote_copy(
            src_ref=half_out.at[slot], dst_ref=half_in.at[slot],
            send_sem=ex_send.at[slot], recv_sem=ex_recv.at[slot],
            device_id=(g, sib), device_id_type=MESH,
        )
        exchange.start()

        def self_half(which, values):
            hi, lo = split(values)
            cs[:, :LANES] = hi
            cs[:, LANES:] = lo
            return product(bhi.at[which], blo.at[which], cs[...])

        fresh[...] = raw[step] + self_half(core, unpack(coef, half, lanes) * spec[core])
        h, length = record(step, finish_sums(slot, second))
        scale = jnp.broadcast_to(1.0 / length, (1, LANES))
        hrows[...] = jnp.broadcast_to(h, (MSG, LANES))

        @pl.loop(0, points // vrows)
        def _(t):
            rows = pl.ds(pl.multiple_of(t * vrows, 8), vrows)

            def one(i, pair):
                c = hrows[pl.ds(i, 1), :]
                return pair[0] - c * basis[i, rows, :], pair[1] - c * raw[i + 1, rows, :]

            v, z = lax.fori_loop(0, step, one, (raw[step, rows, :], fresh[rows, :]))
            basis[step, rows, :] = v * scale
            fresh[rows, :] = z

        exchange.wait()
        fresh[...] += self_half(1 - core, unpack(half_in[slot], half, lanes) * spec[1 - core])
        for c in sends:
            c.wait()
        rhi, rlo = split(recvrows[slot])
        raw[step + 1] = (fresh[...] + halves(dot_tn(rhi, mixes[...]) + dot_tn(rlo, mixes[...]))) * scale
        return carry

    lax.fori_loop(0, ITERS, body, 0)

    slot = ITERS % 2
    dots(slot, ITERS)
    first = stage1(slot)
    for c in first:
        c.start()
    record(ITERS, finish_sums(slot, relay_sums(slot, first)))

    work = hess[...]
    beta = work[0:1, ITERS : ITERS + 1]
    rows = []
    for k in range(ITERS):
        col = work[:, k : k + 1]
        prods = jnp.sum(col * work, axis=0, keepdims=True)
        row = prods / prods[:, k : k + 1]
        rows.append(jnp.where(lane_ids >= k, row, 0.0))
        work = work - jnp.where(lane_ids >= k, col * row, 0.0)
    y = jnp.where(lane_ids == ITERS, -1.0, jnp.zeros((1, LANES), F32))
    for k in reversed(range(ITERS)):
        value = -jnp.sum(rows[k] * y, axis=1, keepdims=True)
        y = jnp.where(lane_ids == k, value, y)
    answer = y[:, 0:1] * basis[0]
    for k in range(1, ITERS):
        answer = answer + y[:, k : k + 1] * basis[k]
    out[...] = answer.T[:lanes]
    left = work[:, ITERS : ITERS + 1]
    norm = jnp.sqrt(jnp.sum(left * left, axis=0, keepdims=True)) / beta
    res[...] = jnp.broadcast_to(norm, res.shape)


def per_device(groups, patches, right_side, analysis, spectral, near_kernel, near_send, near_target, near_strength):
    cells, comps, points = right_side.shape
    total = near_kernel.shape[0]
    modes = analysis.shape[1]
    lanes = cells * comps
    cap = near_send.shape[-1]
    half = round_up(modes - low_modes(modes), 16)
    near_rows, far_rows = cap * comps, round_up(FAR_CAP * comps, 8)
    blocks, total_rows = blocks_of(groups, near_rows, far_rows)
    side = right_side.transpose(1, 0, 2).reshape(lanes, points)

    vmem = pl.BlockSpec(memory_space=pltpu.VMEM)
    hbm = pl.BlockSpec(memory_space=pl.ANY)
    dma = pltpu.SemaphoreType.DMA
    chips = max(patches // 2, 1)
    main = packed_rows(points)
    pieces = pieces_of(main)
    answer, residual = pl.pallas_call(
        functools.partial(kernel, groups, patches, lanes, blocks),
        out_shape=(
            jax.ShapeDtypeStruct((lanes, points), F32),
            jax.ShapeDtypeStruct((8, LANES), F32),
        ),
        in_specs=[vmem, hbm, vmem, hbm, vmem, vmem, vmem],
        out_specs=(vmem, vmem),
        scratch_shapes=[
            pltpu.VMEM((ITERS + 1, points, LANES), F32),
            pltpu.VMEM((points, LANES), F32),
            pltpu.VMEM((2, patches, main, LANES), F32),
            pltpu.VMEM((ITERS, points, LANES), F32),
            pltpu.VMEM((total, 2 * LANES), BF16),
            pltpu.VMEM((half, 2 * LANES), BF16),
            pltpu.VMEM((points, modes), F32),
            pltpu.VMEM((points, total), F32),
            pltpu.VMEM((2, points, half), F32),
            pltpu.VMEM((2, points, half), F32),
            pltpu.VMEM((2, half, LANES), F32),
            pltpu.VMEM((total_rows, LANES), BF16),
            pltpu.VMEM((total_rows, 2 * LANES), BF16),
            pltpu.VMEM((chips, points, 2 * points), BF16),
            pltpu.VMEM((chips, points, 2 * points), BF16),
            pltpu.VMEM((half, 2 * points), BF16),
            pltpu.VMEM((half, 2 * points), BF16),
            pltpu.VMEM((2, points, half), BF16),
            pltpu.VMEM((2, points, half), BF16),
            pltpu.VMEM((2, packed_rows(half), LANES), F32),
            pltpu.VMEM((2, max(chips - 1, 1), packed_rows(half), LANES), F32),
            pltpu.VMEM((2, packed_rows(half), LANES), F32),
            pltpu.VMEM((2, packed_rows(half), LANES), F32),
            pltpu.VMEM((2, total_rows, points), F32),
            pltpu.VMEM((2, total_rows, points), F32),
            pltpu.VMEM((2, groups, MSG, LANES), F32),
            pltpu.VMEM((2, patches, MSG, LANES), F32),
            pltpu.VMEM((MSG, LANES), F32),
            pltpu.VMEM((MSG, LANES), F32),
            dma((2, chips, pieces)), dma((2, chips, pieces)), dma((2, chips, pieces)), dma((2, chips, pieces)),
            dma((2, groups)), dma((2, groups)), dma((2, patches)), dma((2, patches)),
            dma((2, groups)), dma((2, groups)),
            dma((2, chips)), dma((2, chips)), dma((2,)), dma((2,)), dma((1,)), dma((1,)), dma((2,)),
        ],
        compiler_params=pltpu.CompilerParams(
            collective_id=0, has_side_effects=True, vmem_limit_bytes=60 * 1024 * 1024
        ),
        name="gmres",
    )(side, analysis, spectral, near_kernel.T, near_send[0], near_target[0], near_strength[0])
    return answer.reshape(comps, cells, points).transpose(1, 0, 2), residual[0, 0]


def solution(mesh):
    placed = (
        P("cell", None, "patch"),
        P("patch", None),
        P("cell", None),
        P(None, "patch"),
        P("cell", None, None),
        P("cell", None, None),
        P("cell", None, None),
    )
    return jax.shard_map(
        functools.partial(per_device, mesh.shape["cell"], mesh.shape["patch"]),
        mesh=mesh,
        in_specs=placed,
        out_specs=(P("cell", None, "patch"), P()),
        check_vma=False,
    )
```

```python
import functools

import jax
import jax.numpy as jnp
from jax import lax
from jax.experimental import pallas as pl
from jax.experimental.pallas import tpu as pltpu
from jax.sharding import PartitionSpec as P

ITERS = 8
FAR_CAP = 2
LANES = 128
MSG = 16
F32 = jnp.float32
BF16 = jnp.bfloat16
MESH = pl.DeviceIdType.MESH


def round_up(value, unit):
    return -(-value // unit) * unit


def split(x):
    hi = x.astype(BF16)
    return hi, (x - hi.astype(F32)).astype(BF16)


def halves(x):
    return x[:, :LANES] + x[:, LANES:]


def dot(a, b):
    return jnp.dot(a, b, preferred_element_type=F32)


def product(hi, lo, b):
    rows = hi.shape[0]
    cut = round_up(rows // 2, 16)
    return jnp.concatenate(
        [halves(dot(hi[a:z], b) + dot(lo[a:z], b)) for a, z in ((0, cut), (cut, rows))], 0
    )


def dot_nt(a, b):
    return lax.dot_general(a, b, (((1,), (1,)), ((), ())), preferred_element_type=F32)


def dot_tn(a, b):
    return lax.dot_general(a, b, (((0,), (0,)), ((), ())), preferred_element_type=F32)


def blocks_of(groups, near_rows, far_rows):
    out, at = {}, 0
    for d in sorted(range(groups), key=lambda d: (min(d, groups - d) > 1, d)):
        rows = near_rows if min(d, groups - d) <= 1 else far_rows
        out[d] = (at, rows)
        at += rows
    return out, at


def packed_rows(rows):
    return round_up(rows * 3 // 4, 8)


def pack(dst, x, lanes):
    idle = LANES - lanes
    main = dst.shape[0]
    tail = x.shape[0] - main
    lane = lax.broadcasted_iota(jnp.int32, (1, LANES), 1)
    dst[...] = x[:main]
    for i in range(lanes // idle):
        rows = slice(i * tail, (i + 1) * tail)
        moved = pltpu.roll(x[main:], lanes - idle * i, 1)
        dst[rows, :] = jnp.where(lane >= lanes, moved, x[rows])


def unpack(src, total, lanes):
    idle = LANES - lanes
    main = src.shape[0]
    tail = total - main
    lane = lax.broadcasted_iota(jnp.int32, (1, LANES), 1)
    end = jnp.zeros((tail, LANES), F32)
    for i in range(lanes // idle):
        moved = pltpu.roll(src[i * tail : (i + 1) * tail], (idle * i - lanes) % LANES, 1)
        end = jnp.where((lane >= idle * i) & (lane < idle * (i + 1)), moved, end)
    return jnp.concatenate((jnp.where(lane < lanes, src, 0.0), end), 0)


def low_modes(modes):
    return max(modes // 2 // LANES * LANES, 0)


def cuts_of(points):
    cut = points // 2 // LANES * LANES
    return ((0, cut), (cut, points)) if cut else ((0, points),)


def spans_of(points):
    spans, at = [], 0
    for a, z in cuts_of(points):
        rows = packed_rows(z - a)
        spans.append((at, rows))
        at += rows
    return spans, at


def tile_rows(total, unit, most):
    best = unit
    for rows in range(unit, most + 1, unit):
        if total % rows == 0:
            best = rows
    return best


def kernel(
    groups, patches, lanes, blocks,
    side, analysis, spectral, kernel_t, near_send, near_target, near_strength,
    out, res,
    raw, fresh, packed, basis, vs, cs, astage, kstage, both, pair, spec, sel, mixes,
    khi, klo, ahi, alo, bhi, blo, part_out, part_in, half_out, half_in,
    sendrows, recvrows, msg1, msg2, hess, hrows,
    ag_send, ag_recv, fw_send, fw_recv, s1_send, s1_recv, s2_send, s2_recv, a2_send, a2_recv,
    cf_send, cf_recv, ex_send, ex_recv, sw_send, sw_recv, in_sem,
):
    points = side.shape[1]
    modes = analysis.shape[1]
    cells = spectral.shape[0]
    comps = lanes // cells
    low = low_modes(modes)
    half = spec.shape[1]
    cuts = cuts_of(points)
    spans, _ = spans_of(points)
    pieces = len(cuts)
    width = 2 * points
    g = lax.axis_index("cell")
    p = lax.axis_index("patch")
    core = lax.rem(p, 2)
    chip = p // 2
    sib = p + 1 - 2 * core
    chips = patches // 2

    loads = [
        pltpu.make_async_copy(analysis, astage, in_sem.at[0]),
        pltpu.make_async_copy(kernel_t, kstage, in_sem.at[1]),
    ]
    for c in loads:
        c.start()
    msg1[...] = jnp.zeros_like(msg1)
    barrier = pltpu.get_barrier_semaphore()
    for d in range(1, groups):
        pl.semaphore_signal(barrier, inc=1, device_id=(lax.rem(g + d, groups), p), device_id_type=MESH)
    for d in range(1, patches):
        pl.semaphore_signal(barrier, inc=1, device_id=(g, lax.rem(p + d, patches)), device_id_type=MESH)

    hess[...] = jnp.zeros_like(hess)
    pad = jnp.zeros((LANES - lanes, points), F32)
    raw[0] = jnp.concatenate((side[...], pad), 0).T
    pl.semaphore_wait(barrier, groups + patches - 2)

    def slot_rows(ref, who, rows, fill):
        row = lax.broadcasted_iota(jnp.int32, (rows, ref.shape[1]), 0)
        slot = lax.broadcasted_iota(jnp.int32, (rows, ref.shape[1]), 1)
        count = rows // comps
        hit = (row // comps == slot) & (row < count * comps)
        values = jnp.broadcast_to(ref[pl.ds(who, 1), :].astype(F32), hit.shape)
        found = jnp.sum(jnp.where(hit, values, 0.0), axis=1, keepdims=True)
        return jnp.where(row[:, :1] < count * comps, found, fill)

    def setup():
        lane = lax.broadcasted_iota(jnp.int32, (1, LANES), 1)
        cell = (lane % cells).astype(F32)
        for d in range(groups):
            at, rows = blocks[d]
            row = lax.broadcasted_iota(jnp.int32, (rows, 1), 0)
            same = (row % comps == lane // cells) & (lane < lanes)
            ahead, behind = lax.rem(g + d, groups), lax.rem(g + groups - d, groups)
            picks = same & (slot_rows(near_send, ahead, rows, -1.0) == cell)
            sel[at : at + rows, :] = jnp.where(picks, 1.0, 0.0).astype(BF16)
            hits = same & (slot_rows(near_target, behind, rows, -1.0) == cell)
            mix = jnp.where(hits, slot_rows(near_strength, behind, rows, 0.0), 0.0)
            mixes[at : at + rows, :LANES], mixes[at : at + rows, LANES:] = split(mix)
        both[...] = jnp.zeros_like(both)
        spec[...] = jnp.zeros_like(spec)
        loads[0].wait()
        both[0, :, :low] = astage[:, :low]
        both[1, :, : modes - low] = astage[:, low:]
        swap = pltpu.make_async_remote_copy(
            src_ref=both.at[1 - core], dst_ref=pair.at[core],
            send_sem=sw_send.at[0], recv_sem=sw_recv.at[0],
            device_id=(g, sib), device_id_type=MESH,
        )
        swap.start()
        each = spectral[...]
        each = jnp.concatenate((each,) * comps + (jnp.zeros((LANES - lanes, modes), F32),), 0).T
        spec[0, :low, :] = each[:low]
        spec[1, : modes - low, :] = each[low:]
        for c in range(2):
            bhi[c], blo[c] = split(both[c])
        loads[1].wait()
        for c in range(chips):
            for a, z in cuts:
                one = kstage[:, c * width + a : c * width + z]
                two = kstage[:, c * width + points + a : c * width + points + z]
                for i, x in enumerate((jnp.where(core == 0, one, two), jnp.where(core == 0, two, one))):
                    at = 2 * a + i * (z - a)
                    khi[c, :, at : at + z - a], klo[c, :, at : at + z - a] = split(x)
        pair[core] = both[core]
        swap.wait()
        parts = [pair[who, a:z] for a, z in cuts for who in (core, 1 - core)]
        ahi[...], alo[...] = split(jnp.concatenate(parts, 0).T)

    def dots(slot, count):
        def one(i, carry):
            msg1[slot, g, pl.ds(i, 1), :] = jnp.sum(basis[i] * raw[count], axis=0, keepdims=True)
            return carry

        lax.fori_loop(0, count, one, 0)
        msg1[slot, g, ITERS : ITERS + 1, :] = jnp.sum(raw[count] * raw[count], axis=0, keepdims=True)

    def stage1(slot):
        return [
            pltpu.make_async_remote_copy(
                src_ref=msg1.at[slot, g], dst_ref=msg1.at[slot, g],
                send_sem=s1_send.at[slot, d], recv_sem=s1_recv.at[slot, d],
                device_id=(lax.rem(g + d, groups), p), device_id_type=MESH,
            )
            for d in range(1, groups)
        ]

    def stage2(slot):
        return [
            pltpu.make_async_remote_copy(
                src_ref=msg2.at[slot, p], dst_ref=msg2.at[slot, p],
                send_sem=s2_send.at[slot, d], recv_sem=s2_recv.at[slot, d],
                device_id=(g, lax.rem(p + d, patches)), device_id_type=MESH,
            )
            for d in range(1, patches)
        ]

    def relay_sums(slot, first):
        for c in first:
            c.wait()
        local = msg1[slot, 0]
        for q in range(1, groups):
            local = local + msg1[slot, q]
        msg2[slot, p] = local
        second = stage2(slot)
        for c in second:
            c.start()
        return second

    def finish_sums(slot, second):
        for c in second:
            c.wait()
        whole = msg2[slot, 0]
        for q in range(1, patches):
            whole = whole + msg2[slot, q]
        return jnp.sum(whole, axis=1, keepdims=True)

    row_ids = lax.broadcasted_iota(jnp.int32, (MSG, 1), 0)
    lane_ids = lax.broadcasted_iota(jnp.int32, (1, LANES), 1)

    def record(step, sums):
        squared = sums[ITERS : ITERS + 1, :]
        h = jnp.where(row_ids < ITERS, sums, 0.0)
        length = jnp.sqrt(squared - jnp.sum(h * h, axis=0, keepdims=True))
        column = jnp.where(row_ids == step, length, h)
        lane = lax.rem(step + ITERS, ITERS + 1)
        hess[...] = jnp.where(lane_ids == lane, column, hess[...])
        return h, length

    vrows = tile_rows(points, 8, 96)

    def body(step, carry):
        slot = lax.rem(step, 2)
        for (a, z), (at, rows) in zip(cuts, spans):
            pack(packed.at[slot, p, pl.ds(at, rows)], raw[step, a:z], lanes)
        own = pltpu.make_async_remote_copy(
            src_ref=packed.at[slot, p], dst_ref=packed.at[slot, p],
            send_sem=ag_send.at[slot, 0, 0], recv_sem=ag_recv.at[slot, 0, 0],
            device_id=(g, sib), device_id_type=MESH,
        )
        cross, forward = [], []
        for n in range(pieces):
            rows = pl.ds(*spans[n])
            for k in range(1, chips):
                cross.append(pltpu.make_async_remote_copy(
                    src_ref=packed.at[slot, p, rows], dst_ref=packed.at[slot, p, rows],
                    send_sem=ag_send.at[slot, k, n], recv_sem=ag_recv.at[slot, k, n],
                    device_id=(g, lax.rem(p + 2 * k, patches)), device_id_type=MESH,
                ))
                src = lax.rem(p + patches - 2 * k, patches)
                forward.append(pltpu.make_async_remote_copy(
                    src_ref=packed.at[slot, src, rows], dst_ref=packed.at[slot, src, rows],
                    send_sem=fw_send.at[slot, k, n], recv_sem=fw_recv.at[slot, k, n],
                    device_id=(g, sib), device_id_type=MESH,
                ))
        for c in cross:
            c.start()
        own.start()
        dots(slot, step)
        first = stage1(slot)
        for c in first:
            c.start()

        pl.when(step == 0)(setup)

        def put(which, n, i, v):
            a, z = cuts[n]
            rows = slice(2 * a + i * (z - a), 2 * a + (i + 1) * (z - a))
            hi, lo = split(v)
            vs[which, rows, :LANES] = hi
            vs[which, rows, LANES:] = lo

        def place(which, n, i):
            who = 2 * which + (core if i == 0 else 1 - core)
            at, rows = spans[n]
            put(which, n, i, unpack(packed[slot, who, at : at + rows], cuts[n][1] - cuts[n][0], lanes))

        for n, (a, z) in enumerate(cuts):
            put(chip, n, 0, raw[step, a:z])
        own.wait()
        for n in range(pieces):
            place(chip, n, 1)
        near = vs[chip]
        pack(part_out.at[slot], product(ahi, alo, near), lanes)
        partials = [
            pltpu.make_async_remote_copy(
                src_ref=part_out.at[slot], dst_ref=part_in.at[slot, k - 1],
                send_sem=cf_send.at[slot, k], recv_sem=cf_recv.at[slot, k],
                device_id=(g, lax.rem(p + 2 * k, patches)), device_id_type=MESH,
            )
            for k in range(1, chips)
        ]
        for c in partials:
            c.start()
        acc = product(khi.at[chip], klo.at[chip], near)
        for n in range(pieces):
            a, z = 2 * cuts[n][0], 2 * cuts[n][1]
            here = [(k, cross[n * (chips - 1) + k - 1], forward[n * (chips - 1) + k - 1]) for k in range(1, chips)]
            for k, c, f in here:
                c.wait()
                f.start()
                place(lax.rem(chip + chips - k, chips), n, 0)
            for k, c, f in here:
                other = lax.rem(chip + chips - k, chips)
                f.wait()
                place(other, n, 1)
                acc = acc + product(khi.at[other, :, a:z], klo.at[other, :, a:z], vs[other, a:z])
        whi, wlo = split(acc)
        sendrows[slot] = dot_nt(sel[...], whi) + dot_nt(sel[...], wlo)
        sends = []
        for d in sorted(range(1, groups), key=lambda d: min(d, groups - d) > 1):
            at, rows = blocks[d]
            sends.append(pltpu.make_async_remote_copy(
                src_ref=sendrows.at[slot, pl.ds(at, rows)], dst_ref=recvrows.at[slot, pl.ds(at, rows)],
                send_sem=a2_send.at[slot, d], recv_sem=a2_recv.at[slot, d],
                device_id=(lax.rem(g + d, groups), p), device_id_type=MESH,
            ))
        for c in sends:
            c.start()
        second = relay_sums(slot, first)
        recvrows[slot, : blocks[0][1], :] = sendrows[slot, : blocks[0][1], :]

        coef = part_out[slot]
        for k, c in enumerate(partials, 1):
            c.wait()
            coef = coef + part_in[slot, k - 1]
        half_out[slot] = coef
        exchange = pltpu.make_async_remote_copy(
            src_ref=half_out.at[slot], dst_ref=half_in.at[slot],
            send_sem=ex_send.at[slot], recv_sem=ex_recv.at[slot],
            device_id=(g, sib), device_id_type=MESH,
        )
        exchange.start()

        def self_half(which, values):
            hi, lo = split(values)
            cs[:, :LANES] = hi
            cs[:, LANES:] = lo
            return product(bhi.at[which], blo.at[which], cs[...])

        fresh[...] = raw[step] + self_half(core, unpack(coef, half, lanes) * spec[core])
        h, length = record(step, finish_sums(slot, second))
        scale = jnp.broadcast_to(1.0 / length, (1, LANES))
        hrows[...] = jnp.broadcast_to(h, (MSG, LANES))

        @pl.loop(0, points // vrows)
        def _(t):
            rows = pl.ds(pl.multiple_of(t * vrows, 8), vrows)

            def one(i, pair):
                c = hrows[pl.ds(i, 1), :]
                return pair[0] - c * basis[i, rows, :], pair[1] - c * raw[i + 1, rows, :]

            v, z = lax.fori_loop(0, step, one, (raw[step, rows, :], fresh[rows, :]))
            basis[step, rows, :] = v * scale
            fresh[rows, :] = z

        exchange.wait()
        fresh[...] += self_half(1 - core, unpack(half_in[slot], half, lanes) * spec[1 - core])
        for c in sends:
            c.wait()
        rhi, rlo = split(recvrows[slot])
        raw[step + 1] = (fresh[...] + halves(dot_tn(rhi, mixes[...]) + dot_tn(rlo, mixes[...]))) * scale
        return carry

    lax.fori_loop(0, ITERS, body, 0)

    slot = ITERS % 2
    dots(slot, ITERS)
    first = stage1(slot)
    for c in first:
        c.start()
    record(ITERS, finish_sums(slot, relay_sums(slot, first)))

    work = hess[...]
    beta = work[0:1, ITERS : ITERS + 1]
    rows = []
    for k in range(ITERS):
        col = work[:, k : k + 1]
        prods = jnp.sum(col * work, axis=0, keepdims=True)
        row = prods / prods[:, k : k + 1]
        rows.append(jnp.where(lane_ids >= k, row, 0.0))
        work = work - jnp.where(lane_ids >= k, col * row, 0.0)
    y = jnp.where(lane_ids == ITERS, -1.0, jnp.zeros((1, LANES), F32))
    for k in reversed(range(ITERS)):
        value = -jnp.sum(rows[k] * y, axis=1, keepdims=True)
        y = jnp.where(lane_ids == k, value, y)
    answer = y[:, 0:1] * basis[0]
    for k in range(1, ITERS):
        answer = answer + y[:, k : k + 1] * basis[k]
    out[...] = answer.T[:lanes]
    left = work[:, ITERS : ITERS + 1]
    norm = jnp.sqrt(jnp.sum(left * left, axis=0, keepdims=True)) / beta
    res[...] = jnp.broadcast_to(norm, res.shape)


def per_device(groups, patches, right_side, analysis, spectral, near_kernel, near_send, near_target, near_strength):
    cells, comps, points = right_side.shape
    total = near_kernel.shape[0]
    modes = analysis.shape[1]
    lanes = cells * comps
    cap = near_send.shape[-1]
    half = round_up(modes - low_modes(modes), 16)
    near_rows, far_rows = cap * comps, round_up(FAR_CAP * comps, 8)
    blocks, total_rows = blocks_of(groups, near_rows, far_rows)
    side = right_side.transpose(1, 0, 2).reshape(lanes, points)

    vmem = pl.BlockSpec(memory_space=pltpu.VMEM)
    hbm = pl.BlockSpec(memory_space=pl.ANY)
    dma = pltpu.SemaphoreType.DMA
    chips = max(patches // 2, 1)
    pieces = len(cuts_of(points))
    _, main = spans_of(points)
    answer, residual = pl.pallas_call(
        functools.partial(kernel, groups, patches, lanes, blocks),
        out_shape=(
            jax.ShapeDtypeStruct((lanes, points), F32),
            jax.ShapeDtypeStruct((8, LANES), F32),
        ),
        in_specs=[vmem, hbm, vmem, hbm, vmem, vmem, vmem],
        out_specs=(vmem, vmem),
        scratch_shapes=[
            pltpu.VMEM((ITERS + 1, points, LANES), F32),
            pltpu.VMEM((points, LANES), F32),
            pltpu.VMEM((2, patches, main, LANES), F32),
            pltpu.VMEM((ITERS, points, LANES), F32),
            pltpu.VMEM((chips, 2 * points, 2 * LANES), BF16),
            pltpu.VMEM((half, 2 * LANES), BF16),
            pltpu.VMEM((points, modes), F32),
            pltpu.VMEM((points, total), F32),
            pltpu.VMEM((2, points, half), F32),
            pltpu.VMEM((2, points, half), F32),
            pltpu.VMEM((2, half, LANES), F32),
            pltpu.VMEM((total_rows, LANES), BF16),
            pltpu.VMEM((total_rows, 2 * LANES), BF16),
            pltpu.VMEM((chips, points, 2 * points), BF16),
            pltpu.VMEM((chips, points, 2 * points), BF16),
            pltpu.VMEM((half, 2 * points), BF16),
            pltpu.VMEM((half, 2 * points), BF16),
            pltpu.VMEM((2, points, half), BF16),
            pltpu.VMEM((2, points, half), BF16),
            pltpu.VMEM((2, packed_rows(half), LANES), F32),
            pltpu.VMEM((2, max(chips - 1, 1), packed_rows(half), LANES), F32),
            pltpu.VMEM((2, packed_rows(half), LANES), F32),
            pltpu.VMEM((2, packed_rows(half), LANES), F32),
            pltpu.VMEM((2, total_rows, points), F32),
            pltpu.VMEM((2, total_rows, points), F32),
            pltpu.VMEM((2, groups, MSG, LANES), F32),
            pltpu.VMEM((2, patches, MSG, LANES), F32),
            pltpu.VMEM((MSG, LANES), F32),
            pltpu.VMEM((MSG, LANES), F32),
            dma((2, chips, pieces)), dma((2, chips, pieces)), dma((2, chips, pieces)), dma((2, chips, pieces)),
            dma((2, groups)), dma((2, groups)), dma((2, patches)), dma((2, patches)),
            dma((2, groups)), dma((2, groups)),
            dma((2, chips)), dma((2, chips)), dma((2,)), dma((2,)), dma((1,)), dma((1,)), dma((2,)),
        ],
        compiler_params=pltpu.CompilerParams(
            collective_id=0, has_side_effects=True, vmem_limit_bytes=60 * 1024 * 1024
        ),
        name="gmres",
    )(side, analysis, spectral, near_kernel.T, near_send[0], near_target[0], near_strength[0])
    return answer.reshape(comps, cells, points).transpose(1, 0, 2), residual[0, 0]


def solution(mesh):
    placed = (
        P("cell", None, "patch"),
        P("patch", None),
        P("cell", None),
        P(None, "patch"),
        P("cell", None, None),
        P("cell", None, None),
        P("cell", None, None),
    )
    return jax.shard_map(
        functools.partial(per_device, mesh.shape["cell"], mesh.shape["patch"]),
        mesh=mesh,
        in_specs=placed,
        out_specs=(P("cell", None, "patch"), P()),
        check_vma=False,
    )
```

```python
import functools

import jax
import jax.numpy as jnp
from jax import lax
from jax.experimental import pallas as pl
from jax.experimental.pallas import tpu as pltpu
from jax.sharding import PartitionSpec as P

ITERS = 8
FAR_CAP = 2
LANES = 128
MSG = 16
F32 = jnp.float32
BF16 = jnp.bfloat16
MESH = pl.DeviceIdType.MESH


def round_up(value, unit):
    return -(-value // unit) * unit


def split(x):
    hi = x.astype(BF16)
    return hi, (x - hi.astype(F32)).astype(BF16)


def halves(x):
    return x[:, :LANES] + x[:, LANES:]


def dot(a, b):
    return jnp.dot(a, b, preferred_element_type=F32)


def product(hi, lo, b):
    rows = hi.shape[0]
    cut = round_up(rows // 2, 16)
    return jnp.concatenate(
        [halves(dot(hi[a:z], b) + dot(lo[a:z], b)) for a, z in ((0, cut), (cut, rows))], 0
    )


def dot_nt(a, b):
    return lax.dot_general(a, b, (((1,), (1,)), ((), ())), preferred_element_type=F32)


def dot_tn(a, b):
    return lax.dot_general(a, b, (((0,), (0,)), ((), ())), preferred_element_type=F32)


def blocks_of(groups, near_rows, far_rows):
    out, at = {}, 0
    for d in sorted(range(groups), key=lambda d: (min(d, groups - d) > 1, d)):
        rows = near_rows if min(d, groups - d) <= 1 else far_rows
        out[d] = (at, rows)
        at += rows
    return out, at


def packed_rows(rows):
    return round_up(rows * 3 // 4, 8)


def pack(dst, x, lanes):
    idle = LANES - lanes
    main = dst.shape[0]
    tail = x.shape[0] - main
    lane = lax.broadcasted_iota(jnp.int32, (1, LANES), 1)
    dst[...] = x[:main]
    for i in range(lanes // idle):
        rows = slice(i * tail, (i + 1) * tail)
        moved = pltpu.roll(x[main:], lanes - idle * i, 1)
        dst[rows, :] = jnp.where(lane >= lanes, moved, x[rows])


def unpack(src, total, lanes):
    idle = LANES - lanes
    main = src.shape[0]
    tail = total - main
    lane = lax.broadcasted_iota(jnp.int32, (1, LANES), 1)
    end = jnp.zeros((tail, LANES), F32)
    for i in range(lanes // idle):
        moved = pltpu.roll(src[i * tail : (i + 1) * tail], (idle * i - lanes) % LANES, 1)
        end = jnp.where((lane >= idle * i) & (lane < idle * (i + 1)), moved, end)
    return jnp.concatenate((jnp.where(lane < lanes, src, 0.0), end), 0)


def low_modes(modes):
    return max(modes // 2 // LANES * LANES, 0)


def tiles_of(blocks, points):
    most = max(rows for _, rows in blocks.values())
    tiles, at = {}, 0
    for d, (_, rows) in blocks.items():
        count = rows // 8 * (points // LANES) + (rows == most)
        tiles[d] = (at, count)
        at += count
    return tiles, at


def cuts_of(points):
    cut = points // 2 // LANES * LANES
    return ((0, cut), (cut, points)) if cut else ((0, points),)


def spans_of(points):
    spans, at = [], 0
    for a, z in cuts_of(points):
        rows = packed_rows(z - a)
        spans.append((at, rows))
        at += rows
    return spans, at


def tile_rows(total, unit, most):
    best = unit
    for rows in range(unit, most + 1, unit):
        if total % rows == 0:
            best = rows
    return best


def kernel(
    groups, patches, lanes, blocks,
    side, analysis, spectral, kernel_t, near_send, near_target, near_strength,
    out, res,
    raw, fresh, packed, basis, vs, cs, astage, kstage, both, pair, spec, sel, mixes,
    khi, klo, ahi, alo, bhi, blo, part_out, part_in, half_out, half_in,
    sendt, recvt, recvrows, msg1, msg2, hess, hrows,
    ag_send, ag_recv, fw_send, fw_recv, s1_send, s1_recv, s2_send, s2_recv, a2_send, a2_recv,
    cf_send, cf_recv, ex_send, ex_recv, sw_send, sw_recv, in_sem,
):
    points = side.shape[1]
    modes = analysis.shape[1]
    cells = spectral.shape[0]
    comps = lanes // cells
    low = low_modes(modes)
    half = spec.shape[1]
    cuts = cuts_of(points)
    spans, _ = spans_of(points)
    pieces = len(cuts)
    width = 2 * points
    g = lax.axis_index("cell")
    p = lax.axis_index("patch")
    core = lax.rem(p, 2)
    chip = p // 2
    sib = p + 1 - 2 * core
    chips = patches // 2

    loads = [
        pltpu.make_async_copy(analysis, astage, in_sem.at[0]),
        pltpu.make_async_copy(kernel_t, kstage, in_sem.at[1]),
    ]
    for c in loads:
        c.start()
    msg1[...] = jnp.zeros_like(msg1)
    barrier = pltpu.get_barrier_semaphore()
    for d in range(1, groups):
        pl.semaphore_signal(barrier, inc=1, device_id=(lax.rem(g + d, groups), p), device_id_type=MESH)
    for d in range(1, patches):
        pl.semaphore_signal(barrier, inc=1, device_id=(g, lax.rem(p + d, patches)), device_id_type=MESH)

    hess[...] = jnp.zeros_like(hess)
    pad = jnp.zeros((LANES - lanes, points), F32)
    raw[0] = jnp.concatenate((side[...], pad), 0).T
    pl.semaphore_wait(barrier, groups + patches - 2)

    def slot_rows(ref, who, rows, fill):
        row = lax.broadcasted_iota(jnp.int32, (rows, ref.shape[1]), 0)
        slot = lax.broadcasted_iota(jnp.int32, (rows, ref.shape[1]), 1)
        count = rows // comps
        hit = (row // comps == slot) & (row < count * comps)
        values = jnp.broadcast_to(ref[pl.ds(who, 1), :].astype(F32), hit.shape)
        found = jnp.sum(jnp.where(hit, values, 0.0), axis=1, keepdims=True)
        return jnp.where(row[:, :1] < count * comps, found, fill)

    def setup():
        lane = lax.broadcasted_iota(jnp.int32, (1, LANES), 1)
        cell = (lane % cells).astype(F32)
        for d in range(groups):
            at, rows = blocks[d]
            row = lax.broadcasted_iota(jnp.int32, (rows, 1), 0)
            same = (row % comps == lane // cells) & (lane < lanes)
            ahead, behind = lax.rem(g + d, groups), lax.rem(g + groups - d, groups)
            picks = same & (slot_rows(near_send, ahead, rows, -1.0) == cell)
            sel[at : at + rows, :] = jnp.where(picks, 1.0, 0.0).astype(BF16)
            hits = same & (slot_rows(near_target, behind, rows, -1.0) == cell)
            mix = jnp.where(hits, slot_rows(near_strength, behind, rows, 0.0), 0.0)
            mixes[at : at + rows, :LANES], mixes[at : at + rows, LANES:] = split(mix)
        both[...] = jnp.zeros_like(both)
        spec[...] = jnp.zeros_like(spec)
        loads[0].wait()
        both[0, :, :low] = astage[:, :low]
        both[1, :, : modes - low] = astage[:, low:]
        swap = pltpu.make_async_remote_copy(
            src_ref=both.at[1 - core], dst_ref=pair.at[core],
            send_sem=sw_send.at[0], recv_sem=sw_recv.at[0],
            device_id=(g, sib), device_id_type=MESH,
        )
        swap.start()
        each = spectral[...]
        each = jnp.concatenate((each,) * comps + (jnp.zeros((LANES - lanes, modes), F32),), 0).T
        spec[0, :low, :] = each[:low]
        spec[1, : modes - low, :] = each[low:]
        for c in range(2):
            bhi[c], blo[c] = split(both[c])
        loads[1].wait()
        for c in range(chips):
            for a, z in cuts:
                one = kstage[:, c * width + a : c * width + z]
                two = kstage[:, c * width + points + a : c * width + points + z]
                for i, x in enumerate((jnp.where(core == 0, one, two), jnp.where(core == 0, two, one))):
                    at = 2 * a + i * (z - a)
                    khi[c, :, at : at + z - a], klo[c, :, at : at + z - a] = split(x)
        pair[core] = both[core]
        swap.wait()
        parts = [pair[who, a:z] for a, z in cuts for who in (core, 1 - core)]
        ahi[...], alo[...] = split(jnp.concatenate(parts, 0).T)

    def dots(slot, count):
        def one(i, carry):
            msg1[slot, g, pl.ds(i, 1), :] = jnp.sum(basis[i] * raw[count], axis=0, keepdims=True)
            return carry

        lax.fori_loop(0, count, one, 0)
        msg1[slot, g, ITERS : ITERS + 1, :] = jnp.sum(raw[count] * raw[count], axis=0, keepdims=True)

    def stage1(slot):
        return [
            pltpu.make_async_remote_copy(
                src_ref=msg1.at[slot, g], dst_ref=msg1.at[slot, g],
                send_sem=s1_send.at[slot, d], recv_sem=s1_recv.at[slot, d],
                device_id=(lax.rem(g + d, groups), p), device_id_type=MESH,
            )
            for d in range(1, groups)
        ]

    def stage2(slot):
        return [
            pltpu.make_async_remote_copy(
                src_ref=msg2.at[slot, p], dst_ref=msg2.at[slot, p],
                send_sem=s2_send.at[slot, d], recv_sem=s2_recv.at[slot, d],
                device_id=(g, lax.rem(p + d, patches)), device_id_type=MESH,
            )
            for d in range(1, patches)
        ]

    def relay_sums(slot, first):
        for c in first:
            c.wait()
        local = msg1[slot, 0]
        for q in range(1, groups):
            local = local + msg1[slot, q]
        msg2[slot, p] = local
        second = stage2(slot)
        for c in second:
            c.start()
        return second

    def finish_sums(slot, second):
        for c in second:
            c.wait()
        whole = msg2[slot, 0]
        for q in range(1, patches):
            whole = whole + msg2[slot, q]
        return jnp.sum(whole, axis=1, keepdims=True)

    row_ids = lax.broadcasted_iota(jnp.int32, (MSG, 1), 0)
    lane_ids = lax.broadcasted_iota(jnp.int32, (1, LANES), 1)

    def record(step, sums):
        squared = sums[ITERS : ITERS + 1, :]
        h = jnp.where(row_ids < ITERS, sums, 0.0)
        length = jnp.sqrt(squared - jnp.sum(h * h, axis=0, keepdims=True))
        column = jnp.where(row_ids == step, length, h)
        lane = lax.rem(step + ITERS, ITERS + 1)
        hess[...] = jnp.where(lane_ids == lane, column, hess[...])
        return h, length

    vrows = tile_rows(points, 8, 96)
    base = points // LANES * LANES
    tail = points - base
    wide_tiles = base // LANES
    tiles, _ = tiles_of(blocks, points)
    row8 = lax.broadcasted_iota(jnp.int32, (8, LANES), 0)
    keep = lax.broadcasted_iota(jnp.int32, (8, LANES), 1) // tail == row8

    def body(step, carry):
        slot = lax.rem(step, 2)
        for (a, z), (at, rows) in zip(cuts, spans):
            pack(packed.at[slot, p, pl.ds(at, rows)], raw[step, a:z], lanes)
        own = pltpu.make_async_remote_copy(
            src_ref=packed.at[slot, p], dst_ref=packed.at[slot, p],
            send_sem=ag_send.at[slot, 0, 0], recv_sem=ag_recv.at[slot, 0, 0],
            device_id=(g, sib), device_id_type=MESH,
        )
        cross, forward = [], []
        for n in range(pieces):
            rows = pl.ds(*spans[n])
            for k in range(1, chips):
                cross.append(pltpu.make_async_remote_copy(
                    src_ref=packed.at[slot, p, rows], dst_ref=packed.at[slot, p, rows],
                    send_sem=ag_send.at[slot, k, n], recv_sem=ag_recv.at[slot, k, n],
                    device_id=(g, lax.rem(p + 2 * k, patches)), device_id_type=MESH,
                ))
                src = lax.rem(p + patches - 2 * k, patches)
                forward.append(pltpu.make_async_remote_copy(
                    src_ref=packed.at[slot, src, rows], dst_ref=packed.at[slot, src, rows],
                    send_sem=fw_send.at[slot, k, n], recv_sem=fw_recv.at[slot, k, n],
                    device_id=(g, sib), device_id_type=MESH,
                ))
        for c in cross:
            c.start()
        own.start()
        dots(slot, step)
        first = stage1(slot)
        for c in first:
            c.start()

        pl.when(step == 0)(setup)

        def put(which, n, i, v):
            a, z = cuts[n]
            rows = slice(2 * a + i * (z - a), 2 * a + (i + 1) * (z - a))
            hi, lo = split(v)
            vs[which, rows, :LANES] = hi
            vs[which, rows, LANES:] = lo

        def place(which, n, i):
            who = 2 * which + (core if i == 0 else 1 - core)
            at, rows = spans[n]
            put(which, n, i, unpack(packed[slot, who, at : at + rows], cuts[n][1] - cuts[n][0], lanes))

        for n, (a, z) in enumerate(cuts):
            put(chip, n, 0, raw[step, a:z])
        own.wait()
        for n in range(pieces):
            place(chip, n, 1)
        near = vs[chip]
        pack(part_out.at[slot], product(ahi, alo, near), lanes)
        partials = [
            pltpu.make_async_remote_copy(
                src_ref=part_out.at[slot], dst_ref=part_in.at[slot, k - 1],
                send_sem=cf_send.at[slot, k], recv_sem=cf_recv.at[slot, k],
                device_id=(g, lax.rem(p + 2 * k, patches)), device_id_type=MESH,
            )
            for k in range(1, chips)
        ]
        for c in partials:
            c.start()
        acc = product(khi.at[chip], klo.at[chip], near)
        for n in range(pieces):
            a, z = 2 * cuts[n][0], 2 * cuts[n][1]
            here = [(k, cross[n * (chips - 1) + k - 1], forward[n * (chips - 1) + k - 1]) for k in range(1, chips)]
            for k, c, f in here:
                c.wait()
                f.start()
                place(lax.rem(chip + chips - k, chips), n, 0)
            for k, c, f in here:
                other = lax.rem(chip + chips - k, chips)
                f.wait()
                place(other, n, 1)
                acc = acc + product(khi.at[other, :, a:z], klo.at[other, :, a:z], vs[other, a:z])
        whi, wlo = split(jnp.concatenate((acc[:base],) + (acc[base:],) * (LANES // tail), 0))
        picked = dot_nt(sel[...], whi) + dot_nt(sel[...], wlo)
        ends = [
            jnp.sum(jnp.where(keep, picked[r : r + 8, base:], 0.0), axis=0, keepdims=True)
            for r in range(0, picked.shape[0], 8)
        ]
        for d in range(groups):
            at, rows = blocks[d]
            first_tile, count = tiles[d]
            for i in range(rows // 8):
                for c in range(wide_tiles):
                    v = picked[at + 8 * i : at + 8 * i + 8, c * LANES : (c + 1) * LANES]
                    if c == 0 and count == wide_tiles:
                        v = jnp.where(row8 == 7, ends[at // 8], v)
                    sendt[slot, first_tile + i * wide_tiles + c] = v
            if count > rows // 8 * wide_tiles:
                extra = jnp.zeros((8, LANES), F32)
                for i in range(rows // 8):
                    extra = jnp.where(row8 == i, ends[at // 8 + i], extra)
                sendt[slot, first_tile + count - 1] = extra
        sends = []
        for d in sorted(range(1, groups), key=lambda d: min(d, groups - d) > 1):
            part = pl.ds(*tiles[d])
            sends.append(pltpu.make_async_remote_copy(
                src_ref=sendt.at[slot, part], dst_ref=recvt.at[slot, part],
                send_sem=a2_send.at[slot, d], recv_sem=a2_recv.at[slot, d],
                device_id=(lax.rem(g + d, groups), p), device_id_type=MESH,
            ))
        for c in sends:
            c.start()
        second = relay_sums(slot, first)
        own_tiles = slice(tiles[0][0], tiles[0][0] + tiles[0][1])
        recvt[slot, own_tiles] = sendt[slot, own_tiles]

        coef = part_out[slot]
        for k, c in enumerate(partials, 1):
            c.wait()
            coef = coef + part_in[slot, k - 1]
        half_out[slot] = coef
        exchange = pltpu.make_async_remote_copy(
            src_ref=half_out.at[slot], dst_ref=half_in.at[slot],
            send_sem=ex_send.at[slot], recv_sem=ex_recv.at[slot],
            device_id=(g, sib), device_id_type=MESH,
        )
        exchange.start()

        def self_half(which, values):
            hi, lo = split(values)
            cs[:, :LANES] = hi
            cs[:, LANES:] = lo
            return product(bhi.at[which], blo.at[which], cs[...])

        fresh[...] = raw[step] + self_half(core, unpack(coef, half, lanes) * spec[core])
        h, length = record(step, finish_sums(slot, second))
        scale = jnp.broadcast_to(1.0 / length, (1, LANES))
        hrows[...] = jnp.broadcast_to(h, (MSG, LANES))

        @pl.loop(0, points // vrows)
        def _(t):
            rows = pl.ds(pl.multiple_of(t * vrows, 8), vrows)

            def one(i, pair):
                c = hrows[pl.ds(i, 1), :]
                return pair[0] - c * basis[i, rows, :], pair[1] - c * raw[i + 1, rows, :]

            v, z = lax.fori_loop(0, step, one, (raw[step, rows, :], fresh[rows, :]))
            basis[step, rows, :] = v * scale
            fresh[rows, :] = z

        exchange.wait()
        fresh[...] += self_half(1 - core, unpack(half_in[slot], half, lanes) * spec[1 - core])
        for c in sends:
            c.wait()
        for d in range(groups):
            at, rows = blocks[d]
            first_tile, count = tiles[d]
            for i in range(rows // 8):
                here = slice(at + 8 * i, at + 8 * i + 8)
                for c in range(wide_tiles):
                    recvrows[here, c * LANES : (c + 1) * LANES] = recvt[slot, first_tile + i * wide_tiles + c]
                if count == wide_tiles:
                    end = recvt[slot, first_tile, 7:8, :]
                else:
                    end = recvt[slot, first_tile + count - 1, i : i + 1, :]
                recvrows[here, base:] = jnp.where(keep, jnp.broadcast_to(end, (8, LANES)), 0.0)
        rhi, rlo = split(recvrows[...])
        added = halves(dot_tn(rhi, mixes[...]) + dot_tn(rlo, mixes[...]))
        last = added[base : base + tail]
        for k in range(1, LANES // tail):
            last = last + added[base + k * tail : base + (k + 1) * tail]
        raw[step + 1, :base] = (fresh[:base] + added[:base]) * scale
        raw[step + 1, base:] = (fresh[base:] + last) * scale
        return carry

    lax.fori_loop(0, ITERS, body, 0)

    slot = ITERS % 2
    dots(slot, ITERS)
    first = stage1(slot)
    for c in first:
        c.start()
    record(ITERS, finish_sums(slot, relay_sums(slot, first)))

    work = hess[...]
    beta = work[0:1, ITERS : ITERS + 1]
    rows = []
    for k in range(ITERS):
        col = work[:, k : k + 1]
        prods = jnp.sum(col * work, axis=0, keepdims=True)
        row = prods / prods[:, k : k + 1]
        rows.append(jnp.where(lane_ids >= k, row, 0.0))
        work = work - jnp.where(lane_ids >= k, col * row, 0.0)
    y = jnp.where(lane_ids == ITERS, -1.0, jnp.zeros((1, LANES), F32))
    for k in reversed(range(ITERS)):
        value = -jnp.sum(rows[k] * y, axis=1, keepdims=True)
        y = jnp.where(lane_ids == k, value, y)
    answer = y[:, 0:1] * basis[0]
    for k in range(1, ITERS):
        answer = answer + y[:, k : k + 1] * basis[k]
    out[...] = answer.T[:lanes]
    left = work[:, ITERS : ITERS + 1]
    norm = jnp.sqrt(jnp.sum(left * left, axis=0, keepdims=True)) / beta
    res[...] = jnp.broadcast_to(norm, res.shape)


def per_device(groups, patches, right_side, analysis, spectral, near_kernel, near_send, near_target, near_strength):
    cells, comps, points = right_side.shape
    total = near_kernel.shape[0]
    modes = analysis.shape[1]
    lanes = cells * comps
    cap = near_send.shape[-1]
    half = round_up(modes - low_modes(modes), 16)
    near_rows, far_rows = cap * comps, round_up(FAR_CAP * comps, 8)
    blocks, total_rows = blocks_of(groups, near_rows, far_rows)
    _, tile_count = tiles_of(blocks, points)
    side = right_side.transpose(1, 0, 2).reshape(lanes, points)

    vmem = pl.BlockSpec(memory_space=pltpu.VMEM)
    hbm = pl.BlockSpec(memory_space=pl.ANY)
    dma = pltpu.SemaphoreType.DMA
    chips = max(patches // 2, 1)
    pieces = len(cuts_of(points))
    _, main = spans_of(points)
    answer, residual = pl.pallas_call(
        functools.partial(kernel, groups, patches, lanes, blocks),
        out_shape=(
            jax.ShapeDtypeStruct((lanes, points), F32),
            jax.ShapeDtypeStruct((8, LANES), F32),
        ),
        in_specs=[vmem, hbm, vmem, hbm, vmem, vmem, vmem],
        out_specs=(vmem, vmem),
        scratch_shapes=[
            pltpu.VMEM((ITERS + 1, points, LANES), F32),
            pltpu.VMEM((points, LANES), F32),
            pltpu.VMEM((2, patches, main, LANES), F32),
            pltpu.VMEM((ITERS, points, LANES), F32),
            pltpu.VMEM((chips, 2 * points, 2 * LANES), BF16),
            pltpu.VMEM((half, 2 * LANES), BF16),
            pltpu.VMEM((points, modes), F32),
            pltpu.VMEM((points, total), F32),
            pltpu.VMEM((2, points, half), F32),
            pltpu.VMEM((2, points, half), F32),
            pltpu.VMEM((2, half, LANES), F32),
            pltpu.VMEM((total_rows, LANES), BF16),
            pltpu.VMEM((total_rows, 2 * LANES), BF16),
            pltpu.VMEM((chips, points, 2 * points), BF16),
            pltpu.VMEM((chips, points, 2 * points), BF16),
            pltpu.VMEM((half, 2 * points), BF16),
            pltpu.VMEM((half, 2 * points), BF16),
            pltpu.VMEM((2, points, half), BF16),
            pltpu.VMEM((2, points, half), BF16),
            pltpu.VMEM((2, packed_rows(half), LANES), F32),
            pltpu.VMEM((2, max(chips - 1, 1), packed_rows(half), LANES), F32),
            pltpu.VMEM((2, packed_rows(half), LANES), F32),
            pltpu.VMEM((2, packed_rows(half), LANES), F32),
            pltpu.VMEM((2, tile_count, 8, LANES), F32),
            pltpu.VMEM((2, tile_count, 8, LANES), F32),
            pltpu.VMEM((total_rows, round_up(points, LANES)), F32),
            pltpu.VMEM((2, groups, MSG, LANES), F32),
            pltpu.VMEM((2, patches, MSG, LANES), F32),
            pltpu.VMEM((MSG, LANES), F32),
            pltpu.VMEM((MSG, LANES), F32),
            dma((2, chips, pieces)), dma((2, chips, pieces)), dma((2, chips, pieces)), dma((2, chips, pieces)),
            dma((2, groups)), dma((2, groups)), dma((2, patches)), dma((2, patches)),
            dma((2, groups)), dma((2, groups)),
            dma((2, chips)), dma((2, chips)), dma((2,)), dma((2,)), dma((1,)), dma((1,)), dma((2,)),
        ],
        compiler_params=pltpu.CompilerParams(
            collective_id=0, has_side_effects=True, vmem_limit_bytes=60 * 1024 * 1024
        ),
        name="gmres",
    )(side, analysis, spectral, near_kernel.T, near_send[0], near_target[0], near_strength[0])
    return answer.reshape(comps, cells, points).transpose(1, 0, 2), residual[0, 0]


def solution(mesh):
    placed = (
        P("cell", None, "patch"),
        P("patch", None),
        P("cell", None),
        P(None, "patch"),
        P("cell", None, None),
        P("cell", None, None),
        P("cell", None, None),
    )
    return jax.shard_map(
        functools.partial(per_device, mesh.shape["cell"], mesh.shape["patch"]),
        mesh=mesh,
        in_specs=placed,
        out_specs=(P("cell", None, "patch"), P()),
        check_vma=False,
    )
```
